128 devices in a mesh: aux: 32 (over x, y, core), pair: 4 (over z).
Axes of the slice: x: 4, y: 4, z: 4, core: 2. Of those that a mesh axis runs over, the one named last changes fastest.
Arguments:
- three_center: bfloat16 [8, 32, 32, 8192], P('pair', None, None, 'aux'), may hold values from -6 to 6
- pair_index: int32 [2, 8], replicated, may hold values from 0 to 31, as said below
- green_occ: bfloat16 [1024, 1024], replicated, may hold values from -0.0625 to 0.0625
- green_virt: bfloat16 [1024, 1024], replicated, may hold values from -0.0625 to 0.0625
- coupling: int32 [32, 32], replicated, may hold values 0 or 1
Outputs:
- polarizability: float32 [8192, 8192], P('aux', 'pair')
The draws below stay inside these ranges and needn't reach their ends.
Inputs may be any that keep to these rules, and one draw needn't show every extreme that they name: The 8 pairs (pair_index[0, k], pair_index[1, k]) are distinct block pairs.
All inputs are finite; a program needn't handle non-finite values.
Results may differ from the reference program's by a relative error of at most 0.015.
Values may be sent and summed in bfloat16 or wider, within the bound.
A program may use at most 128 MiB of HBM per device.

```python
import jax
import jax.numpy as jnp
from jax import lax

BS = 32
PA = 8192
NB = 32
NPR_DEV = 2
NGROUPS = 4
NPAIRS = 8
NBAS = 1024


def draw_pair_index(key, part):
    first_key = jax.random.fold_in(key, 11)
    second_key = jax.random.fold_in(key, 12)
    forced = (NB - 1) * NB
    pair_codes = jax.random.permutation(first_key, NB * NB - 1)[:NPAIRS - 1].astype(jnp.int32)
    pair_codes = pair_codes + (pair_codes >= forced).astype(jnp.int32)
    pair_codes = jnp.concatenate([jnp.full((1,), forced, jnp.int32), pair_codes])
    pair_codes = pair_codes[jax.random.permutation(second_key, NPAIRS)]
    return jnp.stack([pair_codes // NB, pair_codes % NB]).astype(jnp.int32)


def plant(result, stream_key, smallest, high):
    longest = result.shape.index(max(result.shape))
    spots = []
    for shift in (0, 1):
        where = [jax.random.randint(jax.random.fold_in(stream_key, axis), (), 0, length) for axis, length in enumerate(result.shape)]
        where[longest] = (where[longest] + shift) % result.shape[longest]
        spots.append(tuple(where))
    return result.at[spots[0]].set(smallest).at[spots[1]].set(high)


def levels(own_key, shape, pieces, smallest, largest):
    def one(position, parts):
        steps = jax.random.uniform(jax.random.fold_in(jax.random.fold_in(own_key, 6), position), (parts,), jnp.float32, smallest / len(pieces), largest / len(pieces))
        return jnp.repeat(jnp.exp(steps), shape[position] // parts).reshape((-1,) + (1,) * (len(shape) - position - 1))

    level = one(*pieces[0])
    for cut in pieces[1:]:
        level = level * one(*cut)
    return level


def scatter_about(rng, dims, width, limit, pieces=(), dtype=jnp.bfloat16):
    level = levels(rng, dims, pieces, -0.22, 0.18) if pieces else 1.0
    values = jax.random.normal(rng, dims, jnp.float32) * width * level
    return jnp.minimum(jnp.maximum(values, -limit), limit).astype(dtype)


def setup_inputs(seed: int = 0) -> dict:
    splits = jax.random.split(jax.random.key(seed), 6)
    return {
        "three_center": scatter_about(splits[0], (NPAIRS, BS, BS, PA), 1.0, 6.0, ((0, 4), (3, 32))),
        "pair_index": draw_pair_index(jax.random.fold_in(splits[5], 71), 0),
        "green_occ": scatter_about(splits[2], (NBAS, NBAS), (NPAIRS * BS * BS) ** -0.5, 0.0625),
        "green_virt": scatter_about(splits[3], (NBAS, NBAS), (NPAIRS * BS * BS) ** -0.5, 0.0625),
        "coupling": plant((jax.random.randint(splits[4], (NB, NB), 0, 3) < 2).astype(jnp.int32), jax.random.fold_in(splits[4], 1), 0, 1),
    }


def block_of(matrix, row_block, column_block):
    return lax.dynamic_slice(matrix, (row_block * BS, column_block * BS), (BS, BS))


def reference(three_center, pair_index, green_occ, green_virt, coupling):
    row_blocks = pair_index[0]
    col_blocks = pair_index[1]

    def contract(target):
        target_row = row_blocks[target]
        target_col = col_blocks[target]

        def add_source(running_sum, source):
            source_row = row_blocks[source]
            source_col = col_blocks[source]
            weight = (coupling[source_row, target_row] * coupling[source_col, target_col]).astype(jnp.float32)
            occ_block = block_of(green_occ, source_row, target_row).astype(jnp.float32)
            virt_block = block_of(green_virt, source_col, target_col).astype(jnp.float32)
            tensor_block = three_center[source].astype(jnp.float32).reshape(BS, BS * PA)
            occupied = jnp.dot(occ_block.T, tensor_block, preferred_element_type=jnp.float32).astype(jnp.bfloat16)
            virtual = jnp.einsum('nlp,ls->nsp', occupied.reshape(BS, BS, PA).astype(jnp.float32), virt_block)
            return running_sum + weight * virtual, None

        running_sum, _ = lax.scan(add_source, jnp.zeros((BS, BS, PA), jnp.float32), jnp.arange(NPAIRS))
        return running_sum.astype(jnp.bfloat16)

    contracted = lax.map(contract, jnp.arange(NPAIRS))
    flat_contracted = contracted.reshape(NGROUPS, NPR_DEV * BS * BS, PA)
    flat_tensor = three_center.reshape(NGROUPS, NPR_DEV * BS * BS, PA)

    def group_add(running_sum, group):
        left_side = flat_contracted[group].astype(jnp.float32)
        right_side = flat_tensor[group].astype(jnp.float32)
        group_part = lax.dot_general(left_side, right_side, (((0,), (0,)), ((), ())), preferred_element_type=jnp.float32)
        rounded = lax.optimization_barrier(group_part.astype(jnp.bfloat16))
        return running_sum + rounded.astype(jnp.float32), None

    polarizability, _ = lax.scan(group_add, jnp.zeros((PA, PA), jnp.float32), jnp.arange(NGROUPS))
    return polarizability
```

```python
import functools

import jax
import jax.numpy as jnp
from jax import lax
from jax.experimental import pallas as pl
from jax.experimental.pallas import tpu as pltpu
from jax.sharding import PartitionSpec as P

MESH = pl.DeviceIdType.MESH
RING = 4
CHUNKS = 2
Y_OFFSET = (0, 3, 1, 2)


def polarizability_kernel(
    pair_ref, coup_ref, t_ref, occ_hbm, virt_hbm, o_ref,
    occ, virt, tz, tq, ee, vv, acc, ct, d_send, d_half, d_in, d_own, r_buf,
    send_sem, recv_sem, local_sem,
):
    kdim, width = t_ref.shape
    chunk = width // CHUNKS
    block = 32
    square = block * block
    half = kdim // 2
    n_pairs = pair_ref.shape[1]
    owned = n_pairs // RING

    aux = lax.axis_index("aux")
    z = lax.axis_index("pair")
    core = lax.rem(aux, 2)
    y = lax.rem(aux // 2, RING)
    x = aux // (2 * RING)

    def at_x(s):
        return {"aux": (lax.rem(x + s, RING) * RING + y) * 2 + core}

    def at_y(s):
        return {"aux": (x * RING + lax.rem(y + s, RING)) * 2 + core}

    def at_z(s):
        return {"pair": lax.rem(z + s, RING)}

    partner = {"aux": aux + 1 - 2 * core}

    counter = [0]

    def remote(src, dst, device):
        i = counter[0]
        counter[0] += 1
        return pltpu.make_async_remote_copy(
            src_ref=src, dst_ref=dst, send_sem=send_sem.at[i], recv_sem=recv_sem.at[i],
            device_id=device, device_id_type=MESH,
        )

    local_counter = [0]

    def local(src, dst):
        i = local_counter[0]
        local_counter[0] += 1
        return pltpu.make_async_copy(src, dst, local_sem.at[i])

    cols = [pl.ds(h * chunk, chunk) for h in range(CHUNKS)]
    z_plus = [remote(t_ref.at[:, cols[h]], tz.at[h, 0], at_z(1)) for h in range(CHUNKS)]
    z_minus = [remote(t_ref.at[:, cols[h]], tz.at[h, 1], at_z(3)) for h in range(CHUNKS)]
    lo, hi = pl.ds(0, half), pl.ds(half, half)
    zf_plus = [remote(tz.at[h, 0, lo], tz.at[h, 2, lo], at_z(1)) for h in range(CHUNKS)]
    zf_minus = [remote(tz.at[h, 1, hi], tz.at[h, 2, hi], at_z(3)) for h in range(CHUNKS)]

    x_plus = remote(t_ref, tq.at[3, core], at_x(1))
    x_minus = remote(t_ref, tq.at[1, core], at_x(3))
    xf_plus = remote(tq.at[3, core, lo], tq.at[2, core, lo], at_x(1))
    xf_minus = remote(tq.at[1, core, hi], tq.at[2, core, hi], at_x(3))
    core_copy = [remote(t_ref if o == 0 else tq.at[o, core], tq.at[o, core], partner) for o in range(RING)]

    def yrows(slot, part=0, parts=1):
        return pl.ds(slot * chunk + part * (chunk // parts), chunk // parts)

    y_plus = [remote(ct.at[h, yrows(0)], ct.at[h, yrows(1)], at_y(1)) for h in range(CHUNKS)]
    y_minus = [remote(ct.at[h, yrows(0)], ct.at[h, yrows(2)], at_y(3)) for h in range(CHUNKS)]
    yf_plus = [remote(ct.at[h, yrows(1, 0, 2)], ct.at[h, yrows(3, 0, 2)], at_y(1)) for h in range(CHUNKS)]
    yf_minus = [remote(ct.at[h, yrows(2, 1, 2)], ct.at[h, yrows(3, 1, 2)], at_y(3)) for h in range(CHUNKS)]

    half_plus = [remote(d_send.at[h, 1, 0], d_half.at[h, 0], at_z(1)) for h in range(CHUNKS)]
    half_minus = [remote(d_send.at[h, 1, 1], d_half.at[h, 1], at_z(3)) for h in range(CHUNKS)]
    d_plus = [[remote(d_send.at[h, 0, c], d_in.at[h, 0, c], at_z(1)) for c in range(2)] for h in range(CHUNKS)]
    d_minus = [[remote(d_send.at[h, 2, c], d_in.at[h, 1, c], at_z(3)) for c in range(2)] for h in range(CHUNKS)]

    wide = 2 * width
    ocols = pl.ds(pl.multiple_of(y * wide, wide), wide)
    out_copy = [
        [
            remote(r_buf.at[h, yrows(s)], o_ref.at[cols[h], ocols], at_y(Y_OFFSET[s]))
            for s in range(1, RING)
        ]
        for h in range(CHUNKS)
    ]
    out_own = [local(r_buf.at[h, yrows(0)], o_ref.at[cols[h], ocols]) for h in range(CHUNKS)]
    keep = local(t_ref, tq.at[0, core])
    load_occ = local(occ_hbm, occ)
    load_virt = local(virt_hbm, virt)

    load_occ.start()
    load_virt.start()
    keep.start()

    barrier = pltpu.get_barrier_semaphore()
    greeted = [at_x(1), at_x(3), at_y(1), at_y(2), at_y(3), at_z(1), at_z(3), partner]
    for device in greeted:
        pl.semaphore_signal(barrier, inc=1, device_id=device, device_id_type=MESH)
    pl.semaphore_wait(barrier, len(greeted))

    z_plus[0].start()
    z_minus[0].start()
    x_plus.start()
    x_minus.start()
    core_copy[0].start()

    load_occ.wait()
    load_virt.wait()

    def indices(which, positions):
        return [pair_ref[which, position] for position in positions]

    sources = range(n_pairs)
    targets = [z * owned + t for t in range(owned)]

    def onehot(starts, width, step):
        row = lax.broadcasted_iota(jnp.int32, (block, width), 0)
        offset = lax.broadcasted_iota(jnp.int32, (block, width), 1) - row * step
        parts = [(offset == start).astype(jnp.float32).astype(jnp.bfloat16) for start in starts]
        return jnp.concatenate(parts, axis=0)

    def outer(left, right):
        return lax.dot_general(left, right, (((1,), (1,)), ((), ())), preferred_element_type=jnp.float32)

    def select(matrix, which):
        size = matrix.shape[1]
        pick = onehot([i * block for i in indices(which, sources)], size, 1)
        rows = jnp.dot(pick, matrix[...], preferred_element_type=jnp.float32).astype(jnp.bfloat16)
        return outer(onehot([i * block for i in indices(which, targets)], size, 1), rows)

    coupling = coup_ref[...].astype(jnp.float32).astype(jnp.bfloat16)

    def kept(which):
        size = coupling.shape[1]
        pick = onehot(indices(which, sources), size, 0)
        rows = jnp.dot(pick, coupling, preferred_element_type=jnp.float32).astype(jnp.bfloat16)
        return outer(onehot(indices(which, targets), size, 0), rows)

    occ_t = (select(occ, 0) * kept(0) * kept(1)).astype(jnp.bfloat16)
    virt_t = select(virt, 1).astype(jnp.bfloat16)

    def expand(k, carry):
        row = lax.broadcasted_iota(jnp.int32, (n_pairs * block, square), 0)
        lane = lax.broadcasted_iota(jnp.int32, (n_pairs * block, square), 1)
        spread = (row == k * block + lane // block).astype(jnp.float32).astype(jnp.bfloat16)
        tiled = (row == k * block + lane % block).astype(jnp.float32).astype(jnp.bfloat16)
        ee[k] = jnp.dot(occ_t, spread, preferred_element_type=jnp.float32)
        vv[k] = jnp.dot(virt_t, tiled, preferred_element_type=jnp.float32)
        return carry

    lax.fori_loop(0, n_pairs, expand, 0)

    acc[...] = jnp.zeros_like(acc)

    def mix(h, source_z, load):
        def step(i, carry):
            kk = i // 8
            t = lax.rem(i // 4, 2)
            part = lax.rem(i, 4)
            k = source_z * owned + kk
            first = pl.multiple_of(t * block + part * 8, 8)
            left = ee[k, pl.ds(first, 8), :]
            right = vv[k, pl.ds(pl.multiple_of(t * block, block), block), :]
            rows = [(left[j : j + 1, :] * right).astype(jnp.bfloat16) for j in range(8)]
            matrix = jnp.concatenate(rows, axis=0)
            tensor = load(pl.ds(pl.multiple_of(kk * square, square), square))
            out = pl.ds(pl.multiple_of(part * 8 * block, 8 * block), 8 * block)
            acc[h, t, out, :] += jnp.dot(matrix, tensor, preferred_element_type=jnp.float32)
            return carry

        lax.fori_loop(0, owned * owned * 4, step, 0)

    def finish(h):
        for t in range(owned):
            ct[h, 0:chunk, t * square : (t + 1) * square] = acc[h, t].T.astype(jnp.bfloat16)

    for h in range(CHUNKS):
        mix(h, z, lambda rows, h=h: t_ref[rows, h * chunk : (h + 1) * chunk])

    def z_arrive(h):
        z_plus[h].wait_recv()
        zf_plus[h].start()
        z_minus[h].wait_recv()
        zf_minus[h].start()

    def mix_near(h):
        mix(h, lax.rem(z + 3, RING), lambda rows: tz[h, 0, rows, :])
        mix(h, lax.rem(z + 1, RING), lambda rows: tz[h, 1, rows, :])

    def mix_far(h):
        zf_plus[h].wait_recv()
        zf_minus[h].wait_recv()
        mix(h, lax.rem(z + 2, RING), lambda rows: tz[h, 2, rows, :])
        finish(h)
        y_plus[h].start()
        y_minus[h].start()

    def y_arrive(h):
        y_plus[h].wait_recv()
        yf_plus[h].start()
        y_minus[h].wait_recv()
        yf_minus[h].start()

    z_arrive(0)
    z_plus[1].start()
    z_minus[1].start()
    mix_near(0)
    mix_far(0)
    x_plus.wait_recv()
    xf_plus.start()
    core_copy[3].start()
    x_minus.wait_recv()
    xf_minus.start()
    core_copy[1].start()
    z_arrive(1)
    mix_near(1)
    y_arrive(0)
    mix_far(1)
    xf_plus.wait_recv()
    xf_minus.wait_recv()
    core_copy[2].start()
    keep.wait()
    yf_plus[0].wait_recv()
    yf_minus[0].wait_recv()
    for o in range(RING):
        core_copy[o].wait_recv()

    def product(h, r, store):
        o = lax.rem(z + r + RING - x, RING)

        def step(i, carry):
            c = i // 2
            rows = pl.ds(pl.multiple_of(lax.rem(i, 2) * (2 * chunk), 2 * chunk), 2 * chunk)
            store(c, rows, jnp.dot(ct[h, rows, :], tq[o, c], preferred_element_type=jnp.float32))
            return carry

        lax.fori_loop(0, 4, step, 0)

    def to_send(h, r):
        def store(c, rows, value):
            d_send[h, r - 1, c, rows, :] = value.astype(jnp.bfloat16)

        return store

    def join(h, r, c, j):
        total = d_send[h, r - 1, c].astype(jnp.float32) + d_half[h, j].astype(jnp.float32)
        d_send[h, r - 1, c] = total.astype(jnp.bfloat16)

    def reduce_start(h):
        product(h, 2, to_send(h, 2))
        half_plus[h].start()
        half_minus[h].start()
        product(h, 1, to_send(h, 1))
        d_plus[h][1].start()
        product(h, 3, to_send(h, 3))
        d_minus[h][0].start()
        half_plus[h].wait_recv()
        join(h, 1, 0, 0)
        d_plus[h][0].start()
        half_minus[h].wait_recv()
        join(h, 3, 1, 1)
        d_minus[h][1].start()

        def store(c, rows, value):
            d_own[h, c, rows, :] = value

        product(h, 0, store)

    def reduce_end(h):
        for c in range(2):
            d_plus[h][c].wait_recv()
            d_minus[h][c].wait_recv()
            total = d_own[h, c] + d_in[h, 0, c].astype(jnp.float32) + d_in[h, 1, c].astype(jnp.float32)
            r_buf[h, :, c * width : (c + 1) * width] = total.astype(jnp.bfloat16)
        for copy in out_copy[h]:
            copy.start()
        out_own[h].start()

    reduce_start(0)
    y_arrive(1)
    yf_plus[1].wait_recv()
    yf_minus[1].wait_recv()
    reduce_start(1)
    reduce_end(0)
    reduce_end(1)

    for h in range(CHUNKS):
        for copy in out_copy[h]:
            copy.wait_recv()
        out_own[h].wait()
    sends = [x_plus, x_minus, xf_plus, xf_minus] + core_copy
    for h in range(CHUNKS):
        sends += [z_plus[h], z_minus[h], zf_plus[h], zf_minus[h]]
        sends += [y_plus[h], y_minus[h], yf_plus[h], yf_minus[h]]
        sends += [half_plus[h], half_minus[h]] + d_plus[h] + d_minus[h] + out_copy[h]
    for copy in sends:
        copy.wait_send()


def on_device(three_center, pair_index, green_occ, green_virt, coupling):
    owned, block, _, width = three_center.shape
    kdim = owned * block * block
    chunk = width // CHUNKS
    rows = RING * chunk
    n_pairs = pair_index.shape[1]
    bf16, f32 = jnp.bfloat16, jnp.float32
    part = pl.pallas_call(
        polarizability_kernel,
        out_shape=jax.ShapeDtypeStruct((width, RING * 2 * width), bf16),
        in_specs=[
            pl.BlockSpec(memory_space=pltpu.SMEM),
            pl.BlockSpec(memory_space=pltpu.VMEM),
            pl.BlockSpec(memory_space=pltpu.VMEM),
            pl.BlockSpec(memory_space=pl.ANY),
            pl.BlockSpec(memory_space=pl.ANY),
        ],
        out_specs=pl.BlockSpec(memory_space=pl.ANY),
        scratch_shapes=[
            pltpu.VMEM(green_occ.shape, bf16),
            pltpu.VMEM(green_virt.shape, bf16),
            pltpu.VMEM((CHUNKS, 3, kdim, chunk), bf16),
            pltpu.VMEM((RING, 2, kdim, width), bf16),
            pltpu.VMEM((n_pairs, owned * block, block * block), f32),
            pltpu.VMEM((n_pairs, owned * block, block * block), f32),
            pltpu.VMEM((CHUNKS, owned, block * block, chunk), f32),
            pltpu.VMEM((CHUNKS, rows, kdim), bf16),
            pltpu.VMEM((CHUNKS, 3, 2, rows, width), bf16),
            pltpu.VMEM((CHUNKS, 2, rows, width), bf16),
            pltpu.VMEM((CHUNKS, 2, 2, rows, width), bf16),
            pltpu.VMEM((CHUNKS, 2, rows, width), f32),
            pltpu.VMEM((CHUNKS, rows, 2 * width), bf16),
            pltpu.SemaphoreType.DMA((48,)),
            pltpu.SemaphoreType.DMA((48,)),
            pltpu.SemaphoreType.DMA((5,)),
        ],
        compiler_params=pltpu.CompilerParams(
            collective_id=0, has_side_effects=True, vmem_limit_bytes=56 * 1024 * 1024
        ),
        name="polarizability",
    )(pair_index, coupling, three_center.reshape(kdim, width), green_occ, green_virt)
    return part.astype(f32)


def solution(mesh):
    placed = (P("pair", None, None, "aux"), P(), P(), P(), P())
    return jax.shard_map(
        on_device, mesh=mesh, in_specs=placed, out_specs=P("aux", "pair"), check_vma=False
    )
```

```python
import jax
import jax.numpy as jnp
from jax import lax
from jax.experimental import pallas as pl
from jax.experimental.pallas import tpu as pltpu
from jax.sharding import PartitionSpec as P

MESH = pl.DeviceIdType.MESH
RING = 4
CHUNKS = 2
SUBS = 2
Y_OFFSET = (0, 3, 1, 2)


def polarizability_kernel(
    pair_ref, coup_ref, t_hbm, occ_hbm, virt_hbm, o_ref,
    occ, virt, tz, tq, ee, vv, acc, ct, d_send, d_half, d_in, d_own, r_buf,
    send_sem, recv_sem, local_sem,
):
    kdim, width = t_hbm.shape
    chunk = width // CHUNKS
    sub = chunk // SUBS
    block = 32
    square = block * block
    half = kdim // 2
    n_pairs = pair_ref.shape[1]
    owned = n_pairs // RING
    units = range(CHUNKS * SUBS)

    aux = lax.axis_index("aux")
    z = lax.axis_index("pair")
    core = lax.rem(aux, 2)
    y = lax.rem(aux // 2, RING)
    x = aux // (2 * RING)

    def at_x(s):
        return {"aux": (lax.rem(x + s, RING) * RING + y) * 2 + core}

    def at_y(s):
        return {"aux": (x * RING + lax.rem(y + s, RING)) * 2 + core}

    def at_z(s):
        return {"pair": lax.rem(z + s, RING)}

    partner = {"aux": aux + 1 - 2 * core}

    sends = []

    def remote(src, dst, device):
        i = len(sends)
        copy = pltpu.make_async_remote_copy(
            src_ref=src, dst_ref=dst, send_sem=send_sem.at[i], recv_sem=recv_sem.at[i],
            device_id=device, device_id_type=MESH,
        )
        sends.append(copy)
        return copy

    local_counter = [0]

    def local(src, dst):
        i = local_counter[0]
        local_counter[0] += 1
        return pltpu.make_async_copy(src, dst, local_sem.at[i])

    def start(*copies):
        for copy in copies:
            copy.start()

    def arrive(*copies):
        for copy in copies:
            copy.wait_recv()

    mine = tq.at[0, core]
    lo, hi = pl.ds(0, half), pl.ds(half, half)
    halves = (lo, hi)
    cols = [pl.ds(h * chunk, chunk) for h in range(CHUNKS)]
    z_plus = [[remote(mine.at[p, cols[h]], tz.at[h, 0, p], at_z(1)) for p in halves] for h in range(CHUNKS)]
    z_minus = [[remote(mine.at[p, cols[h]], tz.at[h, 1, p], at_z(3)) for p in halves[::-1]] for h in range(CHUNKS)]
    quarters = [pl.ds(i * (half // 2), half // 2) for i in range(4)]
    zf_plus = [[remote(tz.at[h, 0, q], tz.at[h, 2, q], at_z(1)) for q in quarters[:2]] for h in range(CHUNKS)]
    zf_minus = [[remote(tz.at[h, 1, q], tz.at[h, 2, q], at_z(3)) for q in quarters[2:]] for h in range(CHUNKS)]

    x_plus = [remote(mine.at[p], tq.at[3, core, p], at_x(1)) for p in halves]
    x_minus = [remote(mine.at[p], tq.at[1, core, p], at_x(3)) for p in halves[::-1]]
    xf_plus = [remote(tq.at[3, core, q], tq.at[2, core, q], at_x(1)) for q in quarters[:2]]
    xf_minus = [remote(tq.at[1, core, q], tq.at[2, core, q], at_x(3)) for q in quarters[2:]]

    def to_core(o, p):
        return remote(tq.at[o, core, p], tq.at[o, core, p], partner)

    core_own = to_core(0, pl.ds(0, kdim))
    core_plus = [to_core(3, p) for p in halves]
    core_minus = [to_core(1, p) for p in halves[::-1]]
    core_far = [(to_core(2, quarters[q]), to_core(2, quarters[2 + q])) for q in range(2)]

    def yrows(slot, part=0, parts=1):
        return pl.ds(slot * sub + part * (sub // parts), sub // parts)

    y_plus = [remote(ct.at[u, yrows(0)], ct.at[u, yrows(1)], at_y(1)) for u in units]
    y_minus = [remote(ct.at[u, yrows(0)], ct.at[u, yrows(2)], at_y(3)) for u in units]
    yf_plus = [remote(ct.at[u, yrows(1, 0, 2)], ct.at[u, yrows(3, 0, 2)], at_y(1)) for u in units]
    yf_minus = [remote(ct.at[u, yrows(2, 1, 2)], ct.at[u, yrows(3, 1, 2)], at_y(3)) for u in units]

    half_plus = [remote(d_send.at[u, 1, 0], d_half.at[u, 0], at_z(1)) for u in units]
    half_minus = [remote(d_send.at[u, 1, 1], d_half.at[u, 1], at_z(3)) for u in units]
    d_plus = [[remote(d_send.at[u, 0, c], d_in.at[u, 0, c], at_z(1)) for c in range(2)] for u in units]
    d_minus = [[remote(d_send.at[u, 2, c], d_in.at[u, 1, c], at_z(3)) for c in range(2)] for u in units]

    wide = 2 * width
    ocols = pl.ds(pl.multiple_of(y * wide, wide), wide)
    orows = [pl.ds(u * sub, sub) for u in units]
    out_copy = [
        [remote(r_buf.at[u, yrows(s)], o_ref.at[orows[u], ocols], at_y(Y_OFFSET[s])) for s in range(1, RING)]
        for u in units
    ]
    out_own = [local(r_buf.at[u, yrows(0)], o_ref.at[orows[u], ocols]) for u in units]
    keep = local(t_hbm, mine)
    load_occ = local(occ_hbm, occ)
    load_virt = local(virt_hbm, virt)

    start(keep, load_occ, load_virt)

    barrier = pltpu.get_barrier_semaphore()
    greeted = [at_x(1), at_x(3), at_y(1), at_y(2), at_y(3), at_z(1), at_z(3), partner]
    for device in greeted:
        pl.semaphore_signal(barrier, inc=1, device_id=device, device_id_type=MESH)
    pl.semaphore_wait(barrier, len(greeted))

    keep.wait()
    for p in range(2):
        start(z_plus[0][p], z_minus[0][p])
    for p in range(2):
        start(x_plus[p], x_minus[p])
    start(core_own)

    load_occ.wait()
    load_virt.wait()

    def indices(which, positions):
        return [pair_ref[which, position] for position in positions]

    sources = range(n_pairs)
    targets = [z * owned + t for t in range(owned)]

    def onehot(starts, width, step):
        row = lax.broadcasted_iota(jnp.int32, (block, width), 0)
        offset = lax.broadcasted_iota(jnp.int32, (block, width), 1) - row * step
        parts = [(offset == start).astype(jnp.float32).astype(jnp.bfloat16) for start in starts]
        return jnp.concatenate(parts, axis=0)

    def outer(left, right):
        return lax.dot_general(left, right, (((1,), (1,)), ((), ())), preferred_element_type=jnp.float32)

    def select(matrix, which):
        size = matrix.shape[1]
        pick = onehot([i * block for i in indices(which, sources)], size, 1)
        rows = jnp.dot(pick, matrix[...], preferred_element_type=jnp.float32).astype(jnp.bfloat16)
        return outer(onehot([i * block for i in indices(which, targets)], size, 1), rows)

    coupling = coup_ref[...].astype(jnp.float32).astype(jnp.bfloat16)

    def kept(which):
        size = coupling.shape[1]
        pick = onehot(indices(which, sources), size, 0)
        rows = jnp.dot(pick, coupling, preferred_element_type=jnp.float32).astype(jnp.bfloat16)
        return outer(onehot(indices(which, targets), size, 0), rows)

    occ_t = (select(occ, 0) * kept(0) * kept(1)).astype(jnp.bfloat16)
    virt_t = select(virt, 1).astype(jnp.bfloat16)

    def expand(k, carry):
        row = lax.broadcasted_iota(jnp.int32, (n_pairs * block, square), 0)
        lane = lax.broadcasted_iota(jnp.int32, (n_pairs * block, square), 1)
        spread = (row == k * block + lane // block).astype(jnp.float32).astype(jnp.bfloat16)
        tiled = (row == k * block + lane % block).astype(jnp.float32).astype(jnp.bfloat16)
        ee[k] = jnp.dot(occ_t, spread, preferred_element_type=jnp.float32)
        vv[k] = jnp.dot(virt_t, tiled, preferred_element_type=jnp.float32)
        return carry

    lax.fori_loop(0, n_pairs, expand, 0)

    def matrix(k, t, part, lanes):
        left = ee[k, pl.ds(pl.multiple_of(t * block + part * 8, 8), 8), lanes]
        right = vv[k, pl.ds(pl.multiple_of(t * block, block), block), lanes]
        rows = [(left[j : j + 1, :] * right).astype(jnp.bfloat16) for j in range(8)]
        return jnp.concatenate(rows, axis=0)

    def mix(sources, store, lanes=slice(0, square)):
        def step(i, carry):
            t, part = i // 4, lax.rem(i, 4)
            total = None
            for k, load in sources:
                term = jnp.dot(matrix(k, t, part, lanes), load(), preferred_element_type=jnp.float32)
                total = term if total is None else total + term
            store(t, pl.ds(pl.multiple_of(part * 8 * block, 8 * block), 8 * block), total)
            return carry

        lax.fori_loop(0, owned * 4, step, 0)

    def pair(offset, kk):
        return lax.rem(z + offset, RING) * owned + kk

    def store_own(t, rows, total):
        for h in range(CHUNKS):
            acc[h, t, rows, :] = total[:, h * chunk : (h + 1) * chunk]

    def add_to(h):
        def store(t, rows, total):
            acc[h, t, rows, :] += total

        return store

    def arrived(h, slot, kk):
        return lambda: tz[h, slot, kk * half : (kk + 1) * half, :]

    mix([(pair(0, kk), lambda kk=kk: tq[0, core, kk * half : (kk + 1) * half, :]) for kk in range(2)], store_own)

    def mix_near(h, p):
        mix([(pair(3, p), arrived(h, 0, p)), (pair(1, 1 - p), arrived(h, 1, 1 - p))], add_to(h))

    def mix_far(h, q):
        arrive(zf_plus[h][q], zf_minus[h][q])
        size = half // 2
        sources = [
            (pair(2, kk), lambda first=kk * half + q * size: tz[h, 2, first : first + size, :]) for kk in range(2)
        ]
        mix(sources, add_to(h), slice(q * size, (q + 1) * size))

    def finish(h):
        for t in range(owned):
            columns = acc[h, t].T.astype(jnp.bfloat16)
            for v in range(SUBS):
                ct[h * SUBS + v, 0:sub, t * square : (t + 1) * square] = columns[v * sub : (v + 1) * sub]
        start(y_plus[h * SUBS], y_minus[h * SUBS])

    def product(u, r, store):
        o = lax.rem(z + r + RING - x, RING)

        def step(c, carry):
            store(c, jnp.dot(ct[u], tq[o, c], preferred_element_type=jnp.float32))
            return carry

        lax.fori_loop(0, 2, step, 0)

    def product_send(u, r):
        def store(c, value):
            d_send[u, r - 1, c] = value.astype(jnp.bfloat16)

        product(u, r, store)

    def product_own(u):
        def store(c, value):
            d_own[u, c] = value

        product(u, 0, store)

    def product_far(u):
        product_send(u, 2)
        start(half_plus[u], half_minus[u])

    def product_near(u):
        product_send(u, 1)
        start(d_plus[u][1])
        product_send(u, 3)
        start(d_minus[u][0])

    def join(u):
        for copy, r, c, j, onward in ((half_plus[u], 1, 0, 0, d_plus[u][0]), (half_minus[u], 3, 1, 1, d_minus[u][1])):
            arrive(copy)
            total = d_send[u, r - 1, c].astype(jnp.float32) + d_half[u, j].astype(jnp.float32)
            d_send[u, r - 1, c] = total.astype(jnp.bfloat16)
            start(onward)

    def reduce_end(u):
        for c in range(2):
            arrive(d_plus[u][c], d_minus[u][c])
            total = d_own[u, c] + d_in[u, 0, c].astype(jnp.float32) + d_in[u, 1, c].astype(jnp.float32)
            r_buf[u, :, c * width : (c + 1) * width] = total.astype(jnp.bfloat16)
        start(*out_copy[u])
        start(out_own[u])

    def y_pass(u):
        arrive(y_plus[u])
        start(yf_plus[u])
        arrive(y_minus[u])
        start(yf_minus[u])
        if u % SUBS < SUBS - 1:
            start(y_plus[u + 1], y_minus[u + 1])

    def z_pass(h):
        arrive(z_plus[h][0])
        start(*zf_plus[h])
        arrive(z_minus[h][0])
        start(*zf_minus[h])

    z_pass(0)
    for p in range(2):
        start(z_plus[1][p], z_minus[1][p])
    mix_near(0, 0)
    arrive(x_plus[0])
    start(*xf_plus, core_plus[0])
    arrive(x_minus[0])
    start(*xf_minus, core_minus[0])
    arrive(z_plus[0][1], z_minus[0][1])
    mix_near(0, 1)
    mix_far(0, 0)
    mix_far(0, 1)
    finish(0)
    z_pass(1)
    arrive(x_plus[1], x_minus[1])
    start(core_plus[1], core_minus[1])
    mix_near(1, 0)
    y_pass(0)
    arrive(z_plus[1][1], z_minus[1][1])
    mix_near(1, 1)
    arrive(xf_plus[0], xf_minus[0])
    start(*core_far[0])
    mix_far(1, 0)
    arrive(xf_plus[1], xf_minus[1])
    start(*core_far[1])
    arrive(yf_plus[0], yf_minus[0])
    y_pass(1)
    arrive(core_own, *core_plus, *core_minus, *core_far[0], *core_far[1])
    product_far(0)
    mix_far(1, 1)
    finish(1)
    product_near(0)
    join(0)
    arrive(yf_plus[1], yf_minus[1])
    product_far(1)
    product_near(1)
    y_pass(2)
    join(1)
    product_own(0)
    product_own(1)
    arrive(yf_plus[2], yf_minus[2])
    product_far(2)
    product_near(2)
    y_pass(3)
    join(2)
    reduce_end(0)
    product_own(2)
    reduce_end(1)
    arrive(yf_plus[3], yf_minus[3])
    product_far(3)
    product_near(3)
    join(3)
    product_own(3)
    reduce_end(2)
    reduce_end(3)

    for u in units:
        arrive(*out_copy[u])
        out_own[u].wait()
    for copy in sends:
        copy.wait_send()


def on_device(three_center, pair_index, green_occ, green_virt, coupling):
    owned, block, _, width = three_center.shape
    kdim = owned * block * block
    chunk = width // CHUNKS
    sub = chunk // SUBS
    units = CHUNKS * SUBS
    rows = RING * sub
    n_pairs = pair_index.shape[1]
    bf16, f32 = jnp.bfloat16, jnp.float32
    part = pl.pallas_call(
        polarizability_kernel,
        out_shape=jax.ShapeDtypeStruct((width, RING * 2 * width), bf16),
        in_specs=[
            pl.BlockSpec(memory_space=pltpu.SMEM),
            pl.BlockSpec(memory_space=pltpu.VMEM),
            pl.BlockSpec(memory_space=pl.ANY),
            pl.BlockSpec(memory_space=pl.ANY),
            pl.BlockSpec(memory_space=pl.ANY),
        ],
        out_specs=pl.BlockSpec(memory_space=pl.ANY),
        scratch_shapes=[
            pltpu.VMEM(green_occ.shape, bf16),
            pltpu.VMEM(green_virt.shape, bf16),
            pltpu.VMEM((CHUNKS, 3, kdim, chunk), bf16),
            pltpu.VMEM((RING, 2, kdim, width), bf16),
            pltpu.VMEM((n_pairs, owned * block, block * block), f32),
            pltpu.VMEM((n_pairs, owned * block, block * block), f32),
            pltpu.VMEM((CHUNKS, owned, block * block, chunk), f32),
            pltpu.VMEM((units, rows, kdim), bf16),
            pltpu.VMEM((units, 3, 2, rows, width), bf16),
            pltpu.VMEM((units, 2, rows, width), bf16),
            pltpu.VMEM((units, 2, 2, rows, width), bf16),
            pltpu.VMEM((units, 2, rows, width), f32),
            pltpu.VMEM((units, rows, 2 * width), bf16),
            pltpu.SemaphoreType.DMA((96,)),
            pltpu.SemaphoreType.DMA((96,)),
            pltpu.SemaphoreType.DMA((8,)),
        ],
        compiler_params=pltpu.CompilerParams(
            collective_id=0, has_side_effects=True, vmem_limit_bytes=56 * 1024 * 1024
        ),
        name="polarizability",
    )(pair_index, coupling, three_center.reshape(kdim, width), green_occ, green_virt)
    return part.astype(f32)


def solution(mesh):
    placed = (P("pair", None, None, "aux"), P(), P(), P(), P())
    return jax.shard_map(
        on_device, mesh=mesh, in_specs=placed, out_specs=P("aux", "pair"), check_vma=False
    )
```

```python
import jax
import jax.numpy as jnp
from jax import lax
from jax.experimental import pallas as pl
from jax.experimental.pallas import tpu as pltpu
from jax.sharding import PartitionSpec as P

MESH = pl.DeviceIdType.MESH
RING = 4
CHUNKS = 2
SUBS = 2
Y_OFFSET = (0, 3, 1, 2)


def polarizability_kernel(
    pair_ref, coup_ref, t_hbm, occ_hbm, virt_hbm, o_ref,
    occ, virt, tz, tq, ee, vv, acc, ct, d_send, d_half, d_in, d_own, r_buf,
    send_sem, recv_sem, local_sem,
):
    kdim, width = t_hbm.shape
    chunk = width // CHUNKS
    sub = chunk // SUBS
    block = 32
    square = block * block
    half = kdim // 2
    n_pairs = pair_ref.shape[1]
    owned = n_pairs // RING
    units = range(CHUNKS * SUBS)

    aux = lax.axis_index("aux")
    z = lax.axis_index("pair")
    core = lax.rem(aux, 2)
    y = lax.rem(aux // 2, RING)
    x = aux // (2 * RING)

    def at_x(s):
        return {"aux": (lax.rem(x + s, RING) * RING + y) * 2 + core}

    def at_y(s):
        return {"aux": (x * RING + lax.rem(y + s, RING)) * 2 + core}

    def at_z(s):
        return {"pair": lax.rem(z + s, RING)}

    partner = {"aux": aux + 1 - 2 * core}

    sends = []

    def remote(src, dst, device):
        i = len(sends)
        copy = pltpu.make_async_remote_copy(
            src_ref=src, dst_ref=dst, send_sem=send_sem.at[i], recv_sem=recv_sem.at[i],
            device_id=device, device_id_type=MESH,
        )
        sends.append(copy)
        return copy

    local_counter = [0]

    def local(src, dst):
        i = local_counter[0]
        local_counter[0] += 1
        return pltpu.make_async_copy(src, dst, local_sem.at[i])

    def start(*copies):
        for copy in copies:
            copy.start()

    def arrive(*copies):
        for copy in copies:
            copy.wait_recv()

    mine = tq.at[0, core]
    lo, hi = pl.ds(0, half), pl.ds(half, half)
    halves = (lo, hi)
    cols = [pl.ds(h * chunk, chunk) for h in range(CHUNKS)]
    z_plus = [[remote(mine.at[p, cols[h]], tz.at[h, 0, p], at_z(1)) for p in halves] for h in range(CHUNKS)]
    z_minus = [[remote(mine.at[p, cols[h]], tz.at[h, 1, p], at_z(3)) for p in halves[::-1]] for h in range(CHUNKS)]
    quarters = [pl.ds(i * (half // 2), half // 2) for i in range(4)]
    zf_plus = [[remote(tz.at[h, 0, q], tz.at[h, 2, q], at_z(1)) for q in quarters[:2]] for h in range(CHUNKS)]
    zf_minus = [[remote(tz.at[h, 1, q], tz.at[h, 2, q], at_z(3)) for q in quarters[2:]] for h in range(CHUNKS)]

    x_plus = [remote(mine.at[p], tq.at[3, core, p], at_x(1)) for p in halves]
    x_minus = [remote(mine.at[p], tq.at[1, core, p], at_x(3)) for p in halves[::-1]]
    xf_plus = [remote(tq.at[3, core, q], tq.at[2, core, q], at_x(1)) for q in quarters[:2]]
    xf_minus = [remote(tq.at[1, core, q], tq.at[2, core, q], at_x(3)) for q in quarters[2:]]

    def to_core(o, p):
        return remote(tq.at[o, core, p], tq.at[o, core, p], partner)

    core_own = to_core(0, pl.ds(0, kdim))
    core_plus = [to_core(3, p) for p in halves]
    core_minus = [to_core(1, p) for p in halves[::-1]]
    core_far = [(to_core(2, quarters[q]), to_core(2, quarters[2 + q])) for q in range(2)]

    def yrows(slot, part=0, parts=1):
        return pl.ds(slot * sub + part * (sub // parts), sub // parts)

    y_plus = [[remote(ct.at[u, yrows(0, i, 2)], ct.at[u, yrows(1, i, 2)], at_y(1)) for i in (0, 1)] for u in units]
    y_minus = [[remote(ct.at[u, yrows(0, i, 2)], ct.at[u, yrows(2, i, 2)], at_y(3)) for i in (1, 0)] for u in units]
    yf_plus = [remote(ct.at[u, yrows(1, 0, 2)], ct.at[u, yrows(3, 0, 2)], at_y(1)) for u in units]
    yf_minus = [remote(ct.at[u, yrows(2, 1, 2)], ct.at[u, yrows(3, 1, 2)], at_y(3)) for u in units]

    half_plus = [remote(d_send.at[u, 1, 0], d_half.at[u, 0], at_z(1)) for u in units]
    half_minus = [remote(d_send.at[u, 1, 1], d_half.at[u, 1], at_z(3)) for u in units]
    d_plus = [[remote(d_send.at[u, 0, c], d_in.at[u, 0, c], at_z(1)) for c in range(2)] for u in units]
    d_minus = [[remote(d_send.at[u, 2, c], d_in.at[u, 1, c], at_z(3)) for c in range(2)] for u in units]

    wide = 2 * width
    ocols = pl.ds(pl.multiple_of(y * wide, wide), wide)
    orows = [pl.ds(u * sub, sub) for u in units]
    out_copy = [
        [remote(r_buf.at[u, yrows(s)], o_ref.at[orows[u], ocols], at_y(Y_OFFSET[s])) for s in range(1, RING)]
        for u in units
    ]
    out_own = [local(r_buf.at[u, yrows(0)], o_ref.at[orows[u], ocols]) for u in units]
    keep = local(t_hbm, mine)
    load_occ = local(occ_hbm, occ)
    load_virt = local(virt_hbm, virt)

    start(keep, load_occ, load_virt)

    barrier = pltpu.get_barrier_semaphore()
    greeted = [at_x(1), at_x(3), at_y(1), at_y(2), at_y(3), at_z(1), at_z(3), partner]
    for device in greeted:
        pl.semaphore_signal(barrier, inc=1, device_id=device, device_id_type=MESH)
    pl.semaphore_wait(barrier, len(greeted))

    keep.wait()
    for p in range(2):
        start(z_plus[0][p], z_minus[0][p])
    for p in range(2):
        start(x_plus[p], x_minus[p])
    start(core_own)

    load_occ.wait()
    load_virt.wait()

    def indices(which, positions):
        return [pair_ref[which, position] for position in positions]

    sources = range(n_pairs)
    targets = [z * owned + t for t in range(owned)]

    def onehot(starts, width, step):
        row = lax.broadcasted_iota(jnp.int32, (block, width), 0)
        offset = lax.broadcasted_iota(jnp.int32, (block, width), 1) - row * step
        parts = [(offset == start).astype(jnp.float32).astype(jnp.bfloat16) for start in starts]
        return jnp.concatenate(parts, axis=0)

    def outer(left, right):
        return lax.dot_general(left, right, (((1,), (1,)), ((), ())), preferred_element_type=jnp.float32)

    def select(matrix, which):
        size = matrix.shape[1]
        pick = onehot([i * block for i in indices(which, sources)], size, 1)
        rows = jnp.dot(pick, matrix[...], preferred_element_type=jnp.float32).astype(jnp.bfloat16)
        return outer(onehot([i * block for i in indices(which, targets)], size, 1), rows)

    coupling = coup_ref[...].astype(jnp.float32).astype(jnp.bfloat16)

    def kept(which):
        size = coupling.shape[1]
        pick = onehot(indices(which, sources), size, 0)
        rows = jnp.dot(pick, coupling, preferred_element_type=jnp.float32).astype(jnp.bfloat16)
        return outer(onehot(indices(which, targets), size, 0), rows)

    occ_t = (select(occ, 0) * kept(0) * kept(1)).astype(jnp.bfloat16)
    virt_t = select(virt, 1).astype(jnp.bfloat16)

    def expand(k, carry):
        row = lax.broadcasted_iota(jnp.int32, (n_pairs * block, square), 0)
        lane = lax.broadcasted_iota(jnp.int32, (n_pairs * block, square), 1)
        spread = (row == k * block + lane // block).astype(jnp.float32).astype(jnp.bfloat16)
        tiled = (row == k * block + lane % block).astype(jnp.float32).astype(jnp.bfloat16)
        ee[k] = jnp.dot(occ_t, spread, preferred_element_type=jnp.float32)
        vv[k] = jnp.dot(virt_t, tiled, preferred_element_type=jnp.float32)
        return carry

    lax.fori_loop(0, n_pairs, expand, 0)

    def matrix(k, t, part, lanes):
        left = ee[k, pl.ds(pl.multiple_of(t * block + part * 8, 8), 8), lanes]
        right = vv[k, pl.ds(pl.multiple_of(t * block, block), block), lanes]
        rows = [(left[j : j + 1, :] * right).astype(jnp.bfloat16) for j in range(8)]
        return jnp.concatenate(rows, axis=0)

    def mix(sources, store, lanes=slice(0, square)):
        def step(i, carry):
            t, part = i // 4, lax.rem(i, 4)
            total = None
            for k, load in sources:
                term = jnp.dot(matrix(k, t, part, lanes), load(), preferred_element_type=jnp.float32)
                total = term if total is None else total + term
            store(t, pl.ds(pl.multiple_of(part * 8 * block, 8 * block), 8 * block), total)
            return carry

        lax.fori_loop(0, owned * 4, step, 0)

    def pair(offset, kk):
        return lax.rem(z + offset, RING) * owned + kk

    def store_own(t, rows, total):
        for h in range(CHUNKS):
            acc[h, t, rows, :] = total[:, h * chunk : (h + 1) * chunk]

    def add_to(h):
        def store(t, rows, total):
            acc[h, t, rows, :] += total

        return store

    def arrived(h, slot, kk):
        return lambda: tz[h, slot, kk * half : (kk + 1) * half, :]

    mix([(pair(0, kk), lambda kk=kk: tq[0, core, kk * half : (kk + 1) * half, :]) for kk in range(2)], store_own)

    def mix_near(h, p):
        mix([(pair(3, p), arrived(h, 0, p)), (pair(1, 1 - p), arrived(h, 1, 1 - p))], add_to(h))

    def mix_far(h, q):
        arrive(zf_plus[h][q], zf_minus[h][q])
        size = half // 2
        sources = [
            (pair(2, kk), lambda first=kk * half + q * size: tz[h, 2, first : first + size, :]) for kk in range(2)
        ]
        mix(sources, add_to(h), slice(q * size, (q + 1) * size))

    def y_send(u):
        for p in range(2):
            start(y_plus[u][p], y_minus[u][p])

    def finish(h):
        for t in range(owned):
            columns = acc[h, t].T.astype(jnp.bfloat16)
            for v in range(SUBS):
                ct[h * SUBS + v, 0:sub, t * square : (t + 1) * square] = columns[v * sub : (v + 1) * sub]
        y_send(h * SUBS)

    def product(u, r, store):
        if u == 0:
            far_block(r)
        o = lax.rem(z + r + RING - x, RING)

        def step(c, carry):
            store(c, jnp.dot(ct[u], tq[o, c], preferred_element_type=jnp.float32))
            return carry

        lax.fori_loop(0, 2, step, 0)

    def product_send(u, r):
        def store(c, value):
            d_send[u, r - 1, c] = value.astype(jnp.bfloat16)

        product(u, r, store)

    def product_own(u):
        def store(c, value):
            d_own[u, c] = value

        product(u, 0, store)

    def product_far(u):
        product_send(u, 2)
        start(half_plus[u], half_minus[u])

    def product_near(u):
        product_send(u, 1)
        start(d_plus[u][1])
        product_send(u, 3)
        start(d_minus[u][0])

    def join(u):
        for copy, r, c, j, onward in ((half_plus[u], 1, 0, 0, d_plus[u][0]), (half_minus[u], 3, 1, 1, d_minus[u][1])):
            arrive(copy)
            total = d_send[u, r - 1, c].astype(jnp.float32) + d_half[u, j].astype(jnp.float32)
            d_send[u, r - 1, c] = total.astype(jnp.bfloat16)
            start(onward)

    def reduce_end(u):
        for c in range(2):
            arrive(d_plus[u][c], d_minus[u][c])
            total = d_own[u, c] + d_in[u, 0, c].astype(jnp.float32) + d_in[u, 1, c].astype(jnp.float32)
            r_buf[u, :, c * width : (c + 1) * width] = total.astype(jnp.bfloat16)
        start(*out_copy[u])
        start(out_own[u])

    def y_pass(u):
        arrive(y_plus[u][0])
        start(yf_plus[u])
        arrive(y_minus[u][0])
        start(yf_minus[u])
        if u % SUBS < SUBS - 1:
            y_send(u + 1)

    def y_arrive(u):
        arrive(y_plus[u][1], y_minus[u][1], yf_plus[u], yf_minus[u])

    def far_block(r):
        @pl.when(lax.rem(z + r + RING - x, RING) == 2)
        def _():
            for q in range(2):
                arrive(xf_plus[q], xf_minus[q])
                start(*core_far[q])
            arrive(*core_far[0], *core_far[1])

    def z_pass(h):
        arrive(z_plus[h][0])
        start(*zf_plus[h])
        arrive(z_minus[h][0])
        start(*zf_minus[h])

    z_pass(0)
    for p in range(2):
        start(z_plus[1][p], z_minus[1][p])
    mix_near(0, 0)
    arrive(x_plus[0])
    start(*xf_plus, core_plus[0])
    arrive(x_minus[0])
    start(*xf_minus, core_minus[0])
    arrive(z_plus[0][1], z_minus[0][1])
    mix_near(0, 1)
    mix_far(0, 0)
    mix_far(0, 1)
    finish(0)
    z_pass(1)
    arrive(x_plus[1], x_minus[1])
    start(core_plus[1], core_minus[1])
    mix_near(1, 0)
    y_pass(0)
    arrive(z_plus[1][1], z_minus[1][1])
    mix_near(1, 1)
    y_arrive(0)
    arrive(core_own, *core_plus, *core_minus)
    product_far(0)
    mix_far(1, 0)
    product_near(0)
    y_pass(1)
    mix_far(1, 1)
    finish(1)
    join(0)
    y_arrive(1)
    product_far(1)
    y_pass(2)
    product_near(1)
    join(1)
    product_own(0)
    product_own(1)
    y_arrive(2)
    product_far(2)
    product_near(2)
    y_pass(3)
    join(2)
    reduce_end(0)
    product_own(2)
    reduce_end(1)
    y_arrive(3)
    product_far(3)
    product_near(3)
    join(3)
    product_own(3)
    reduce_end(2)
    reduce_end(3)

    for u in units:
        arrive(*out_copy[u])
        out_own[u].wait()
    for copy in sends:
        copy.wait_send()


def on_device(three_center, pair_index, green_occ, green_virt, coupling):
    owned, block, _, width = three_center.shape
    kdim = owned * block * block
    chunk = width // CHUNKS
    sub = chunk // SUBS
    units = CHUNKS * SUBS
    rows = RING * sub
    n_pairs = pair_index.shape[1]
    bf16, f32 = jnp.bfloat16, jnp.float32
    part = pl.pallas_call(
        polarizability_kernel,
        out_shape=jax.ShapeDtypeStruct((width, RING * 2 * width), bf16),
        in_specs=[
            pl.BlockSpec(memory_space=pltpu.SMEM),
            pl.BlockSpec(memory_space=pltpu.VMEM),
            pl.BlockSpec(memory_space=pl.ANY),
            pl.BlockSpec(memory_space=pl.ANY),
            pl.BlockSpec(memory_space=pl.ANY),
        ],
        out_specs=pl.BlockSpec(memory_space=pl.ANY),
        scratch_shapes=[
            pltpu.VMEM(green_occ.shape, bf16),
            pltpu.VMEM(green_virt.shape, bf16),
            pltpu.VMEM((CHUNKS, 3, kdim, chunk), bf16),
            pltpu.VMEM((RING, 2, kdim, width), bf16),
            pltpu.VMEM((n_pairs, owned * block, block * block), f32),
            pltpu.VMEM((n_pairs, owned * block, block * block), f32),
            pltpu.VMEM((CHUNKS, owned, block * block, chunk), f32),
            pltpu.VMEM((units, rows, kdim), bf16),
            pltpu.VMEM((units, 3, 2, rows, width), bf16),
            pltpu.VMEM((units, 2, rows, width), bf16),
            pltpu.VMEM((units, 2, 2, rows, width), bf16),
            pltpu.VMEM((units, 2, rows, width), f32),
            pltpu.VMEM((units, rows, 2 * width), bf16),
            pltpu.SemaphoreType.DMA((96,)),
            pltpu.SemaphoreType.DMA((96,)),
            pltpu.SemaphoreType.DMA((8,)),
        ],
        compiler_params=pltpu.CompilerParams(
            collective_id=0, has_side_effects=True, vmem_limit_bytes=56 * 1024 * 1024
        ),
        name="polarizability",
    )(pair_index, coupling, three_center.reshape(kdim, width), green_occ, green_virt)
    return part.astype(f32)


def solution(mesh):
    placed = (P("pair", None, None, "aux"), P(), P(), P(), P())
    return jax.shard_map(
        on_device, mesh=mesh, in_specs=placed, out_specs=P("aux", "pair"), check_vma=False
    )
```

```python
import jax
import jax.numpy as jnp
from jax import lax
from jax.experimental import pallas as pl
from jax.experimental.pallas import tpu as pltpu
from jax.sharding import PartitionSpec as P

MESH = pl.DeviceIdType.MESH
RING = 4
CHUNKS = 2
SUBS = 2
Y_OFFSET = (0, 3, 1, 2)


def polarizability_kernel(
    pair_ref, coup_ref, t_hbm, occ_hbm, virt_hbm, o_ref,
    occ, virt, tz, tq, ee, vv, acc, ct, d_send, d_half, d_in, d_own, r_buf,
    send_sem, recv_sem, local_sem,
):
    kdim, width = t_hbm.shape
    chunk = width // CHUNKS
    sub = chunk // SUBS
    block = 32
    square = block * block
    half = kdim // 2
    n_pairs = pair_ref.shape[1]
    owned = n_pairs // RING
    units = range(CHUNKS * SUBS)

    aux = lax.axis_index("aux")
    z = lax.axis_index("pair")
    core = lax.rem(aux, 2)
    y = lax.rem(aux // 2, RING)
    x = aux // (2 * RING)

    def at_x(s):
        return {"aux": (lax.rem(x + s, RING) * RING + y) * 2 + core}

    def at_y(s):
        return {"aux": (x * RING + lax.rem(y + s, RING)) * 2 + core}

    def at_z(s):
        return {"pair": lax.rem(z + s, RING)}

    partner = {"aux": aux + 1 - 2 * core}

    sends = []

    def remote(src, dst, device):
        i = len(sends)
        copy = pltpu.make_async_remote_copy(
            src_ref=src, dst_ref=dst, send_sem=send_sem.at[i], recv_sem=recv_sem.at[i],
            device_id=device, device_id_type=MESH,
        )
        sends.append(copy)
        return copy

    local_counter = [0]

    def local(src, dst):
        i = local_counter[0]
        local_counter[0] += 1
        return pltpu.make_async_copy(src, dst, local_sem.at[i])

    def start(*copies):
        for copy in copies:
            copy.start()

    def arrive(*copies):
        for copy in copies:
            copy.wait_recv()

    mine = tq.at[0, core]
    lo, hi = pl.ds(0, half), pl.ds(half, half)
    halves = (lo, hi)
    cols = [pl.ds(h * chunk, chunk) for h in range(CHUNKS)]
    z_plus = [[remote(mine.at[p, cols[h]], tz.at[h, 0, p], at_z(1)) for p in halves] for h in range(CHUNKS)]
    z_minus = [[remote(mine.at[p, cols[h]], tz.at[h, 1, p], at_z(3)) for p in halves[::-1]] for h in range(CHUNKS)]
    quarters = [pl.ds(i * (half // 2), half // 2) for i in range(4)]
    zf_plus = [[remote(tz.at[h, 0, q], tz.at[h, 2, q], at_z(1)) for q in quarters[:2]] for h in range(CHUNKS)]
    zf_minus = [[remote(tz.at[h, 1, q], tz.at[h, 2, q], at_z(3)) for q in quarters[2:]] for h in range(CHUNKS)]

    x_plus = [remote(mine.at[p], tq.at[3, core, p], at_x(1)) for p in halves]
    x_minus = [remote(mine.at[p], tq.at[1, core, p], at_x(3)) for p in halves[::-1]]
    xf_plus = [remote(tq.at[3, core, q], tq.at[2, core, q], at_x(1)) for q in quarters[:2]]
    xf_minus = [remote(tq.at[1, core, q], tq.at[2, core, q], at_x(3)) for q in quarters[2:]]

    def to_core(o, p):
        return remote(tq.at[o, core, p], tq.at[o, core, p], partner)

    core_own = to_core(0, pl.ds(0, kdim))
    core_plus = [to_core(3, p) for p in halves]
    core_minus = [to_core(1, p) for p in halves[::-1]]
    core_far = [(to_core(2, quarters[q]), to_core(2, quarters[2 + q])) for q in range(2)]

    def yrows(slot, part=0, parts=1):
        return pl.ds(slot * sub + part * (sub // parts), sub // parts)

    y_plus = [[remote(ct.at[u, yrows(0, i, 2)], ct.at[u, yrows(1, i, 2)], at_y(1)) for i in (0, 1)] for u in units]
    y_minus = [[remote(ct.at[u, yrows(0, i, 2)], ct.at[u, yrows(2, i, 2)], at_y(3)) for i in (1, 0)] for u in units]
    yf_plus = [remote(ct.at[u, yrows(1, 0, 2)], ct.at[u, yrows(3, 0, 2)], at_y(1)) for u in units]
    yf_minus = [remote(ct.at[u, yrows(2, 1, 2)], ct.at[u, yrows(3, 1, 2)], at_y(3)) for u in units]

    half_plus = [remote(d_send.at[u, 1, 0], d_half.at[u, 0], at_z(1)) for u in units]
    half_minus = [remote(d_send.at[u, 1, 1], d_half.at[u, 1], at_z(3)) for u in units]
    d_plus = [[remote(d_send.at[u, 0, c], d_in.at[u, 0, c], at_z(1)) for c in range(2)] for u in units]
    d_minus = [[remote(d_send.at[u, 2, c], d_in.at[u, 1, c], at_z(3)) for c in range(2)] for u in units]

    wide = 2 * width
    ocols = pl.ds(pl.multiple_of(y * wide, wide), wide)
    orows = [pl.ds(u * sub, sub) for u in units]
    out_copy = [
        [remote(r_buf.at[u, yrows(s)], o_ref.at[orows[u], ocols], at_y(Y_OFFSET[s])) for s in range(1, RING)]
        for u in units
    ]
    out_own = [local(r_buf.at[u, yrows(0)], o_ref.at[orows[u], ocols]) for u in units]
    keep = local(t_hbm, mine)
    load_occ = local(occ_hbm, occ)
    load_virt = local(virt_hbm, virt)

    start(keep, load_occ, load_virt)

    barrier = pltpu.get_barrier_semaphore()
    greeted = [at_x(1), at_x(3), at_y(1), at_y(2), at_y(3), at_z(1), at_z(3), partner]
    for device in greeted:
        pl.semaphore_signal(barrier, inc=1, device_id=device, device_id_type=MESH)
    pl.semaphore_wait(barrier, len(greeted))

    keep.wait()
    for p in range(2):
        start(z_plus[0][p], z_minus[0][p])
    for p in range(2):
        start(x_plus[p], x_minus[p])
    start(core_own)

    load_occ.wait()
    load_virt.wait()

    def indices(which, positions):
        return [pair_ref[which, position] for position in positions]

    sources = range(n_pairs)
    targets = [z * owned + t for t in range(owned)]

    def onehot(starts, width, step):
        row = lax.broadcasted_iota(jnp.int32, (block, width), 0)
        offset = lax.broadcasted_iota(jnp.int32, (block, width), 1) - row * step
        parts = [(offset == start).astype(jnp.float32).astype(jnp.bfloat16) for start in starts]
        return jnp.concatenate(parts, axis=0)

    def outer(left, right):
        return lax.dot_general(left, right, (((1,), (1,)), ((), ())), preferred_element_type=jnp.float32)

    def select(matrix, which):
        size = matrix.shape[1]
        pick = onehot([i * block for i in indices(which, sources)], size, 1)
        rows = jnp.dot(pick, matrix[...], preferred_element_type=jnp.float32).astype(jnp.bfloat16)
        return outer(onehot([i * block for i in indices(which, targets)], size, 1), rows)

    coupling = coup_ref[...].astype(jnp.float32).astype(jnp.bfloat16)

    def kept(which):
        size = coupling.shape[1]
        pick = onehot(indices(which, sources), size, 0)
        rows = jnp.dot(pick, coupling, preferred_element_type=jnp.float32).astype(jnp.bfloat16)
        return outer(onehot(indices(which, targets), size, 0), rows)

    occ_t = (select(occ, 0) * kept(0) * kept(1)).astype(jnp.bfloat16)
    virt_t = select(virt, 1).astype(jnp.bfloat16)

    def expand(k, carry):
        row = lax.broadcasted_iota(jnp.int32, (n_pairs * block, square), 0)
        lane = lax.broadcasted_iota(jnp.int32, (n_pairs * block, square), 1)
        spread = (row == k * block + lane // block).astype(jnp.float32).astype(jnp.bfloat16)
        tiled = (row == k * block + lane % block).astype(jnp.float32).astype(jnp.bfloat16)
        ee[k] = jnp.dot(occ_t, spread, preferred_element_type=jnp.float32)
        vv[k] = jnp.dot(virt_t, tiled, preferred_element_type=jnp.float32)
        return carry

    lax.fori_loop(0, n_pairs, expand, 0)

    def matrix(k, t, part, lanes):
        left = ee[k, pl.ds(pl.multiple_of(t * block + part * 8, 8), 8), lanes]
        right = vv[k, pl.ds(pl.multiple_of(t * block, block), block), lanes]
        rows = [(left[j : j + 1, :] * right).astype(jnp.bfloat16) for j in range(8)]
        return jnp.concatenate(rows, axis=0)

    def mix(sources, store, lanes=slice(0, square)):
        def step(i, carry):
            t, part = i // 4, lax.rem(i, 4)
            total = None
            for k, load in sources:
                term = jnp.dot(matrix(k, t, part, lanes), load(), preferred_element_type=jnp.float32)
                total = term if total is None else total + term
            store(t, pl.ds(pl.multiple_of(part * 8 * block, 8 * block), 8 * block), total)
            return carry

        lax.fori_loop(0, owned * 4, step, 0)

    def pair(offset, kk):
        return lax.rem(z + offset, RING) * owned + kk

    def store_own(t, rows, total):
        for h in range(CHUNKS):
            acc[h, t, rows, :] = total[:, h * chunk : (h + 1) * chunk]

    def add_to(h):
        def store(t, rows, total):
            acc[h, t, rows, :] += total

        return store

    def arrived(h, slot, kk):
        return lambda: tz[h, slot, kk * half : (kk + 1) * half, :]

    mix([(pair(0, kk), lambda kk=kk: tq[0, core, kk * half : (kk + 1) * half, :]) for kk in range(2)], store_own)

    def mix_near(h, p):
        mix([(pair(3, p), arrived(h, 0, p)), (pair(1, 1 - p), arrived(h, 1, 1 - p))], add_to(h))

    def mix_far(h, q):
        arrive(zf_plus[h][q], zf_minus[h][q])
        size = half // 2
        sources = [
            (pair(2, kk), lambda first=kk * half + q * size: tz[h, 2, first : first + size, :]) for kk in range(2)
        ]
        mix(sources, add_to(h), slice(q * size, (q + 1) * size))

    def y_send(u):
        for p in range(2):
            start(y_plus[u][p], y_minus[u][p])

    def finish(h):
        for t in range(owned):
            columns = acc[h, t].T.astype(jnp.bfloat16)
            for v in range(SUBS):
                ct[h * SUBS + v, 0:sub, t * square : (t + 1) * square] = columns[v * sub : (v + 1) * sub]
        y_send(h * SUBS)

    def product(u, r, store):
        if u == 0:
            far_block(r)
        o = lax.rem(z + r + RING - x, RING)

        def step(c, carry):
            store(c, jnp.dot(ct[u], tq[o, c], preferred_element_type=jnp.float32))
            return carry

        lax.fori_loop(0, 2, step, 0)

    def product_send(u, r):
        def store(c, value):
            d_send[u, r - 1, c] = value.astype(jnp.bfloat16)

        product(u, r, store)

    def product_own(u):
        def store(c, value):
            d_own[u, c] = value

        product(u, 0, store)

    def product_far(u):
        product_send(u, 2)
        start(half_plus[u], half_minus[u])

    def product_near(u):
        product_send(u, 1)
        start(d_plus[u][1])
        product_send(u, 3)
        start(d_minus[u][0])

    def join(u):
        for copy, r, c, j, onward in ((half_plus[u], 1, 0, 0, d_plus[u][0]), (half_minus[u], 3, 1, 1, d_minus[u][1])):
            arrive(copy)
            total = d_send[u, r - 1, c].astype(jnp.float32) + d_half[u, j].astype(jnp.float32)
            d_send[u, r - 1, c] = total.astype(jnp.bfloat16)
            start(onward)

    def reduce_end(u):
        for c in range(2):
            arrive(d_plus[u][c], d_minus[u][c])
            total = d_own[u, c] + d_in[u, 0, c].astype(jnp.float32) + d_in[u, 1, c].astype(jnp.float32)
            r_buf[u, :, c * width : (c + 1) * width] = total.astype(jnp.bfloat16)
        start(*out_copy[u])
        start(out_own[u])

    def y_pass(u):
        arrive(y_plus[u][0])
        start(yf_plus[u])
        arrive(y_minus[u][0])
        start(yf_minus[u])
        if u % SUBS < SUBS - 1:
            y_send(u + 1)

    def y_arrive(u):
        arrive(y_plus[u][1], y_minus[u][1], yf_plus[u], yf_minus[u])

    def far_block(r):
        @pl.when(lax.rem(z + r + RING - x, RING) == 2)
        def _():
            for q in range(2):
                arrive(xf_plus[q], xf_minus[q])
                start(*core_far[q])
            arrive(*core_far[0], *core_far[1])

    def z_pass(h):
        arrive(z_plus[h][0])
        start(*zf_plus[h])
        arrive(z_minus[h][0])
        start(*zf_minus[h])

    z_pass(0)
    for p in range(2):
        start(z_plus[1][p], z_minus[1][p])
    mix_near(0, 0)
    arrive(x_plus[0])
    start(*xf_plus, core_plus[0])
    arrive(x_minus[0])
    start(*xf_minus, core_minus[0])
    arrive(z_plus[0][1], z_minus[0][1])
    mix_near(0, 1)
    mix_far(0, 0)
    mix_far(0, 1)
    finish(0)
    z_pass(1)
    arrive(x_plus[1], x_minus[1])
    start(core_plus[1], core_minus[1])
    mix_near(1, 0)
    y_pass(0)
    arrive(z_plus[1][1], z_minus[1][1])
    mix_near(1, 1)
    y_arrive(0)
    arrive(core_own, *core_plus, *core_minus)
    product_far(0)
    product_near(0)
    y_pass(1)
    mix_far(1, 0)
    mix_far(1, 1)
    finish(1)
    join(0)
    y_arrive(1)
    product_far(1)
    y_pass(2)
    product_near(1)
    join(1)
    product_own(0)
    product_own(1)
    y_arrive(2)
    product_far(2)
    product_near(2)
    y_pass(3)
    join(2)
    reduce_end(0)
    product_own(2)
    reduce_end(1)
    y_arrive(3)
    product_far(3)
    product_near(3)
    reduce_end(2)
    join(3)
    product_own(3)
    reduce_end(3)

    for u in units:
        arrive(*out_copy[u])
        out_own[u].wait()
    for copy in sends:
        copy.wait_send()


def on_device(three_center, pair_index, green_occ, green_virt, coupling):
    owned, block, _, width = three_center.shape
    kdim = owned * block * block
    chunk = width // CHUNKS
    sub = chunk // SUBS
    units = CHUNKS * SUBS
    rows = RING * sub
    n_pairs = pair_index.shape[1]
    bf16, f32 = jnp.bfloat16, jnp.float32
    part = pl.pallas_call(
        polarizability_kernel,
        out_shape=jax.ShapeDtypeStruct((width, RING * 2 * width), bf16),
        in_specs=[
            pl.BlockSpec(memory_space=pltpu.SMEM),
            pl.BlockSpec(memory_space=pltpu.VMEM),
            pl.BlockSpec(memory_space=pl.ANY),
            pl.BlockSpec(memory_space=pl.ANY),
            pl.BlockSpec(memory_space=pl.ANY),
        ],
        out_specs=pl.BlockSpec(memory_space=pl.ANY),
        scratch_shapes=[
            pltpu.VMEM(green_occ.shape, bf16),
            pltpu.VMEM(green_virt.shape, bf16),
            pltpu.VMEM((CHUNKS, 3, kdim, chunk), bf16),
            pltpu.VMEM((RING, 2, kdim, width), bf16),
            pltpu.VMEM((n_pairs, owned * block, block * block), f32),
            pltpu.VMEM((n_pairs, owned * block, block * block), f32),
            pltpu.VMEM((CHUNKS, owned, block * block, chunk), f32),
            pltpu.VMEM((units, rows, kdim), bf16),
            pltpu.VMEM((units, 3, 2, rows, width), bf16),
            pltpu.VMEM((units, 2, rows, width), bf16),
            pltpu.VMEM((units, 2, 2, rows, width), bf16),
            pltpu.VMEM((units, 2, rows, width), f32),
            pltpu.VMEM((units, rows, 2 * width), bf16),
            pltpu.SemaphoreType.DMA((96,)),
            pltpu.SemaphoreType.DMA((96,)),
            pltpu.SemaphoreType.DMA((8,)),
        ],
        compiler_params=pltpu.CompilerParams(
            collective_id=0, has_side_effects=True, vmem_limit_bytes=56 * 1024 * 1024
        ),
        name="polarizability",
    )(pair_index, coupling, three_center.reshape(kdim, width), green_occ, green_virt)
    return part.astype(f32)


def solution(mesh):
    placed = (P("pair", None, None, "aux"), P(), P(), P(), P())
    return jax.shard_map(
        on_device, mesh=mesh, in_specs=placed, out_specs=P("aux", "pair"), check_vma=False
    )
```

```python
import jax
import jax.numpy as jnp
from jax import lax
from jax.experimental import pallas as pl
from jax.experimental.pallas import tpu as pltpu
from jax.sharding import PartitionSpec as P

MESH = pl.DeviceIdType.MESH
RING = 4
CHUNKS = 2
SUBS = 2
Y_OFFSET = (0, 3, 1, 2)


def polarizability_kernel(
    pair_ref, coup_ref, t_hbm, occ_hbm, virt_hbm, o_ref,
    occ, virt, tz, tq, ee, vv, acc, ct, d_send, d_half, d_in, d_own, r_buf,
    send_sem, recv_sem, local_sem,
):
    kdim, width = t_hbm.shape
    chunk = width // CHUNKS
    sub = chunk // SUBS
    block = 32
    square = block * block
    half = kdim // 2
    n_pairs = pair_ref.shape[1]
    owned = n_pairs // RING
    units = range(CHUNKS * SUBS)

    aux = lax.axis_index("aux")
    z = lax.axis_index("pair")
    core = lax.rem(aux, 2)
    y = lax.rem(aux // 2, RING)
    x = aux // (2 * RING)

    def at_x(s):
        return {"aux": (lax.rem(x + s, RING) * RING + y) * 2 + core}

    def at_y(s):
        return {"aux": (x * RING + lax.rem(y + s, RING)) * 2 + core}

    def at_z(s):
        return {"pair": lax.rem(z + s, RING)}

    partner = {"aux": aux + 1 - 2 * core}

    sends = []

    def remote(src, dst, device):
        i = len(sends)
        copy = pltpu.make_async_remote_copy(
            src_ref=src, dst_ref=dst, send_sem=send_sem.at[i], recv_sem=recv_sem.at[i],
            device_id=device, device_id_type=MESH,
        )
        sends.append(copy)
        return copy

    local_counter = [0]

    def local(src, dst):
        i = local_counter[0]
        local_counter[0] += 1
        return pltpu.make_async_copy(src, dst, local_sem.at[i])

    def start(*copies):
        for copy in copies:
            copy.start()

    def arrive(*copies):
        for copy in copies:
            copy.wait_recv()

    mine = tq.at[0, core]
    lo, hi = pl.ds(0, half), pl.ds(half, half)
    halves = (lo, hi)
    cols = [pl.ds(h * chunk, chunk) for h in range(CHUNKS)]
    z_plus = [[remote(mine.at[p, cols[h]], tz.at[h, 0, p], at_z(1)) for p in halves] for h in range(CHUNKS)]
    z_minus = [[remote(mine.at[p, cols[h]], tz.at[h, 1, p], at_z(3)) for p in halves[::-1]] for h in range(CHUNKS)]
    quarters = [pl.ds(i * (half // 2), half // 2) for i in range(4)]
    zf_plus = [[remote(tz.at[h, 0, q], tz.at[h, 2, q], at_z(1)) for q in quarters[:2]] for h in range(CHUNKS)]
    zf_minus = [[remote(tz.at[h, 1, q], tz.at[h, 2, q], at_z(3)) for q in quarters[2:]] for h in range(CHUNKS)]

    x_plus = [remote(mine.at[p], tq.at[3, core, p], at_x(1)) for p in halves]
    x_minus = [remote(mine.at[p], tq.at[1, core, p], at_x(3)) for p in halves[::-1]]
    xf_plus = [remote(tq.at[3, core, q], tq.at[2, core, q], at_x(1)) for q in quarters[:2]]
    xf_minus = [remote(tq.at[1, core, q], tq.at[2, core, q], at_x(3)) for q in quarters[2:]]

    def to_core(o, p):
        return remote(tq.at[o, core, p], tq.at[o, core, p], partner)

    core_own = to_core(0, pl.ds(0, kdim))
    core_plus = [to_core(3, p) for p in halves]
    core_minus = [to_core(1, p) for p in halves[::-1]]
    core_far = [(to_core(2, quarters[q]), to_core(2, quarters[2 + q])) for q in range(2)]

    def yrows(slot, part=0, parts=1):
        return pl.ds(slot * sub + part * (sub // parts), sub // parts)

    y_plus = [[remote(ct.at[u, yrows(0, i, 2)], ct.at[u, yrows(1, i, 2)], at_y(1)) for i in (0, 1)] for u in units]
    y_minus = [[remote(ct.at[u, yrows(0, i, 2)], ct.at[u, yrows(2, i, 2)], at_y(3)) for i in (1, 0)] for u in units]
    yf_plus = [remote(ct.at[u, yrows(1, 0, 2)], ct.at[u, yrows(3, 0, 2)], at_y(1)) for u in units]
    yf_minus = [remote(ct.at[u, yrows(2, 1, 2)], ct.at[u, yrows(3, 1, 2)], at_y(3)) for u in units]

    half_plus = [remote(d_send.at[u, 1, 0], d_half.at[u, 0], at_z(1)) for u in units]
    half_minus = [remote(d_send.at[u, 1, 1], d_half.at[u, 1], at_z(3)) for u in units]
    d_plus = [[remote(d_send.at[u, 0, c], d_in.at[u, 0, c], at_z(1)) for c in range(2)] for u in units]
    d_minus = [[remote(d_send.at[u, 2, c], d_in.at[u, 1, c], at_z(3)) for c in range(2)] for u in units]

    wide = 2 * width
    ocols = pl.ds(pl.multiple_of(y * wide, wide), wide)
    orows = [pl.ds(u * sub, sub) for u in units]
    out_copy = [
        [remote(r_buf.at[u, yrows(s)], o_ref.at[orows[u], ocols], at_y(Y_OFFSET[s])) for s in range(1, RING)]
        for u in units
    ]
    out_own = [local(r_buf.at[u, yrows(0)], o_ref.at[orows[u], ocols]) for u in units]
    keep = local(t_hbm, mine)
    load_occ = local(occ_hbm, occ)
    load_virt = local(virt_hbm, virt)

    start(keep, load_occ, load_virt)

    barrier = pltpu.get_barrier_semaphore()
    greeted = [at_x(1), at_x(3), at_y(1), at_y(2), at_y(3), at_z(1), at_z(3), partner]
    for device in greeted:
        pl.semaphore_signal(barrier, inc=1, device_id=device, device_id_type=MESH)
    keep.wait()
    pl.semaphore_wait(barrier, len(greeted))
    for p in range(2):
        start(z_plus[0][p], z_minus[0][p])
    for p in range(2):
        start(x_plus[p], x_minus[p])
    start(core_own)

    load_occ.wait()
    load_virt.wait()

    def indices(which, positions):
        return [pair_ref[which, position] for position in positions]

    sources = range(n_pairs)
    targets = [z * owned + t for t in range(owned)]

    def onehot(starts, width, step):
        row = lax.broadcasted_iota(jnp.int32, (block, width), 0)
        offset = lax.broadcasted_iota(jnp.int32, (block, width), 1) - row * step
        parts = [(offset == start).astype(jnp.float32).astype(jnp.bfloat16) for start in starts]
        return jnp.concatenate(parts, axis=0)

    def outer(left, right):
        return lax.dot_general(left, right, (((1,), (1,)), ((), ())), preferred_element_type=jnp.float32)

    def select(matrix, which):
        size = matrix.shape[1]
        pick = onehot([i * block for i in indices(which, sources)], size, 1)
        rows = jnp.dot(pick, matrix[...], preferred_element_type=jnp.float32).astype(jnp.bfloat16)
        return outer(onehot([i * block for i in indices(which, targets)], size, 1), rows)

    coupling = coup_ref[...].astype(jnp.float32).astype(jnp.bfloat16)

    def kept(which):
        size = coupling.shape[1]
        pick = onehot(indices(which, sources), size, 0)
        rows = jnp.dot(pick, coupling, preferred_element_type=jnp.float32).astype(jnp.bfloat16)
        return outer(onehot(indices(which, targets), size, 0), rows)

    occ_t = (select(occ, 0) * kept(0) * kept(1)).astype(jnp.bfloat16)
    virt_t = select(virt, 1).astype(jnp.bfloat16)

    def expand(k, carry):
        row = lax.broadcasted_iota(jnp.int32, (n_pairs * block, square), 0)
        lane = lax.broadcasted_iota(jnp.int32, (n_pairs * block, square), 1)
        spread = (row == k * block + lane // block).astype(jnp.float32).astype(jnp.bfloat16)
        tiled = (row == k * block + lane % block).astype(jnp.float32).astype(jnp.bfloat16)
        ee[k] = jnp.dot(occ_t, spread, preferred_element_type=jnp.float32)
        vv[k] = jnp.dot(virt_t, tiled, preferred_element_type=jnp.float32)
        return carry

    lax.fori_loop(0, n_pairs, expand, 0)

    def matrix(k, t, part, lanes):
        left = ee[k, pl.ds(pl.multiple_of(t * block + part * 8, 8), 8), lanes]
        right = vv[k, pl.ds(pl.multiple_of(t * block, block), block), lanes]
        rows = [(left[j : j + 1, :] * right).astype(jnp.bfloat16) for j in range(8)]
        return jnp.concatenate(rows, axis=0)

    def mix(sources, store, lanes=slice(0, square)):
        def step(i, carry):
            t, part = i // 4, lax.rem(i, 4)
            total = None
            for k, load in sources:
                term = jnp.dot(matrix(k, t, part, lanes), load(), preferred_element_type=jnp.float32)
                total = term if total is None else total + term
            store(t, pl.ds(pl.multiple_of(part * 8 * block, 8 * block), 8 * block), total)
            return carry

        lax.fori_loop(0, owned * 4, step, 0)

    def pair(offset, kk):
        return lax.rem(z + offset, RING) * owned + kk

    def store_own(t, rows, total):
        for h in range(CHUNKS):
            acc[h, t, rows, :] = total[:, h * chunk : (h + 1) * chunk]

    def add_to(h):
        def store(t, rows, total):
            acc[h, t, rows, :] += total

        return store

    def arrived(h, slot, kk):
        return lambda: tz[h, slot, kk * half : (kk + 1) * half, :]

    mix([(pair(0, kk), lambda kk=kk: tq[0, core, kk * half : (kk + 1) * half, :]) for kk in range(2)], store_own)

    def mix_near(h, p):
        mix([(pair(3, p), arrived(h, 0, p)), (pair(1, 1 - p), arrived(h, 1, 1 - p))], add_to(h))

    def mix_far(h, q):
        arrive(zf_plus[h][q], zf_minus[h][q])
        size = half // 2
        sources = [
            (pair(2, kk), lambda first=kk * half + q * size: tz[h, 2, first : first + size, :]) for kk in range(2)
        ]
        mix(sources, add_to(h), slice(q * size, (q + 1) * size))

    def y_send(u):
        for p in range(2):
            start(y_plus[u][p], y_minus[u][p])

    def finish(h):
        for t in range(owned):
            columns = acc[h, t].T.astype(jnp.bfloat16)
            for v in range(SUBS):
                ct[h * SUBS + v, 0:sub, t * square : (t + 1) * square] = columns[v * sub : (v + 1) * sub]
        y_send(h * SUBS)

    def product(u, r, store):
        if u == 0:
            far_block(r)
        o = lax.rem(z + r + RING - x, RING)

        def step(c, carry):
            store(c, jnp.dot(ct[u], tq[o, c], preferred_element_type=jnp.float32))
            return carry

        lax.fori_loop(0, 2, step, 0)

    def product_send(u, r):
        def store(c, value):
            d_send[u, r - 1, c] = value.astype(jnp.bfloat16)

        product(u, r, store)

    def product_own(u):
        def store(c, value):
            d_own[u, c] = value

        product(u, 0, store)

    def product_far(u):
        product_send(u, 2)
        start(half_plus[u], half_minus[u])

    def product_near(u):
        product_send(u, 1)
        start(d_plus[u][1])
        product_send(u, 3)
        start(d_minus[u][0])

    def join(u):
        for copy, r, c, j, onward in ((half_plus[u], 1, 0, 0, d_plus[u][0]), (half_minus[u], 3, 1, 1, d_minus[u][1])):
            arrive(copy)
            total = d_send[u, r - 1, c].astype(jnp.float32) + d_half[u, j].astype(jnp.float32)
            d_send[u, r - 1, c] = total.astype(jnp.bfloat16)
            start(onward)

    def reduce_end(u):
        for c in range(2):
            arrive(d_plus[u][c], d_minus[u][c])
            total = d_own[u, c] + d_in[u, 0, c].astype(jnp.float32) + d_in[u, 1, c].astype(jnp.float32)
            r_buf[u, :, c * width : (c + 1) * width] = total.astype(jnp.bfloat16)
        start(*out_copy[u])
        start(out_own[u])

    def y_pass(u):
        arrive(y_plus[u][0])
        start(yf_plus[u])
        arrive(y_minus[u][0])
        start(yf_minus[u])
        if u % SUBS < SUBS - 1:
            y_send(u + 1)

    def y_arrive(u):
        arrive(y_plus[u][1], y_minus[u][1], yf_plus[u], yf_minus[u])

    def far_block(r):
        @pl.when(lax.rem(z + r + RING - x, RING) == 2)
        def _():
            for q in range(2):
                arrive(xf_plus[q], xf_minus[q])
                start(*core_far[q])
            arrive(*core_far[0], *core_far[1])

    def z_pass(h):
        arrive(z_plus[h][0])
        start(*zf_plus[h])
        arrive(z_minus[h][0])
        start(*zf_minus[h])

    z_pass(0)
    for p in range(2):
        start(z_plus[1][p], z_minus[1][p])
    mix_near(0, 0)
    arrive(x_plus[0])
    start(*xf_plus, core_plus[0])
    arrive(x_minus[0])
    start(*xf_minus, core_minus[0])
    arrive(z_plus[0][1], z_minus[0][1])
    mix_near(0, 1)
    mix_far(0, 0)
    mix_far(0, 1)
    finish(0)
    z_pass(1)
    arrive(x_plus[1], x_minus[1])
    start(core_plus[1], core_minus[1])
    mix_near(1, 0)
    y_pass(0)
    arrive(z_plus[1][1], z_minus[1][1])
    mix_near(1, 1)
    y_arrive(0)
    arrive(core_own, *core_plus, *core_minus)
    product_far(0)
    product_near(0)
    y_pass(1)
    mix_far(1, 0)
    mix_far(1, 1)
    finish(1)
    join(0)
    y_arrive(1)
    product_far(1)
    y_pass(2)
    product_near(1)
    join(1)
    product_own(0)
    product_own(1)
    y_arrive(2)
    product_far(2)
    product_near(2)
    y_pass(3)
    join(2)
    y_arrive(3)
    product_far(3)
    reduce_end(0)
    product_near(3)
    reduce_end(1)
    product_own(2)
    join(3)
    reduce_end(2)
    product_own(3)
    reduce_end(3)

    for u in units:
        arrive(*out_copy[u])
        out_own[u].wait()
    for copy in sends:
        copy.wait_send()


def on_device(three_center, pair_index, green_occ, green_virt, coupling):
    owned, block, _, width = three_center.shape
    kdim = owned * block * block
    chunk = width // CHUNKS
    sub = chunk // SUBS
    units = CHUNKS * SUBS
    rows = RING * sub
    n_pairs = pair_index.shape[1]
    bf16, f32 = jnp.bfloat16, jnp.float32
    part = pl.pallas_call(
        polarizability_kernel,
        out_shape=jax.ShapeDtypeStruct((width, RING * 2 * width), bf16),
        in_specs=[
            pl.BlockSpec(memory_space=pltpu.SMEM),
            pl.BlockSpec(memory_space=pltpu.VMEM),
            pl.BlockSpec(memory_space=pl.ANY),
            pl.BlockSpec(memory_space=pl.ANY),
            pl.BlockSpec(memory_space=pl.ANY),
        ],
        out_specs=pl.BlockSpec(memory_space=pl.ANY),
        scratch_shapes=[
            pltpu.VMEM(green_occ.shape, bf16),
            pltpu.VMEM(green_virt.shape, bf16),
            pltpu.VMEM((CHUNKS, 3, kdim, chunk), bf16),
            pltpu.VMEM((RING, 2, kdim, width), bf16),
            pltpu.VMEM((n_pairs, owned * block, block * block), f32),
            pltpu.VMEM((n_pairs, owned * block, block * block), f32),
            pltpu.VMEM((CHUNKS, owned, block * block, chunk), f32),
            pltpu.VMEM((units, rows, kdim), bf16),
            pltpu.VMEM((units, 3, 2, rows, width), bf16),
            pltpu.VMEM((units, 2, rows, width), bf16),
            pltpu.VMEM((units, 2, 2, rows, width), bf16),
            pltpu.VMEM((units, 2, rows, width), f32),
            pltpu.VMEM((units, rows, 2 * width), bf16),
            pltpu.SemaphoreType.DMA((96,)),
            pltpu.SemaphoreType.DMA((96,)),
            pltpu.SemaphoreType.DMA((8,)),
        ],
        compiler_params=pltpu.CompilerParams(
            collective_id=0, has_side_effects=True, vmem_limit_bytes=56 * 1024 * 1024
        ),
        name="polarizability",
    )(pair_index, coupling, three_center.reshape(kdim, width), green_occ, green_virt)
    return part.astype(f32)


def solution(mesh):
    placed = (P("pair", None, None, "aux"), P(), P(), P(), P())
    return jax.shard_map(
        on_device, mesh=mesh, in_specs=placed, out_specs=P("aux", "pair"), check_vma=False
    )
```
